32 devices in a mesh: row: 4 (over z), col: 8 (over y, x, core).
Axes of the slice: x: 2, y: 2, z: 4, core: 2. Of those that a mesh axis runs over, the one named last changes fastest.
Arguments:
- customer_inputs: bfloat16 [32768, 1024], P(('row', 'col')), may hold values from -6 to 6
- candidate_inputs: bfloat16 [32768, 1024], P(('row', 'col')), may hold values from -6 to 6
- affinity_sharpness: bfloat16 [32768], P(('row', 'col')), may hold values from 4 to 40
- correct_candidate_index: int32 [32768], P(('row', 'col')), may hold values from 0 to 4095
- customer_initial_weights: bfloat16 [1024, 512], replicated, may hold values from -0.1875 to 0.1875
- customer_final_weights: bfloat16 [512, 256], replicated, may hold values from -0.25 to 0.25
- candidate_initial_weights: bfloat16 [1024, 512], replicated, may hold values from -0.1875 to 0.1875
- candidate_final_weights: bfloat16 [512, 256], replicated, may hold values from -0.25 to 0.25
Outputs:
- loss: float32 [], replicated
- grad_user_first: float32 [1024, 512], replicated
- grad_user_second: float32 [512, 256], replicated
- grad_item_first: float32 [1024, 512], replicated
- grad_item_second: float32 [512, 256], replicated
The draws below stay inside these ranges and needn't reach their ends.
Inputs may be any that keep to these rules, and one draw needn't show every extreme that they name: correct_candidate_index[u] indexes the items of u's group in the order of the steps.
All inputs are finite; a program needn't handle non-finite values.
Results may differ from the reference program's by a relative error of at most 0.015.
Values may be sent and summed in bfloat16 or wider, within the bound.
A program may use at most 128 MiB of HBM per device.

```python
import math
import jax
import jax.numpy as jnp
from jax import lax

F_IN = 1024
HID = 512
EMB = 256
MEMBERS_PER_CHIP = 1024
GROUP = 4096
CUSTOMER_COUNT = 32768
N_ROW = 4
N_COL = 8


def with_ends(values, rng, least, largest):
    place = [jax.random.randint(jax.random.fold_in(rng, axis), (), 0, length) for axis, length in enumerate(values.shape)]
    main_axis = values.shape.index(max(values.shape))
    next_to = place[:main_axis] + [(place[main_axis] + 1) % values.shape[main_axis]] + place[main_axis + 1:]
    return values.at[tuple(place)].set(least).at[tuple(next_to)].set(largest)


def level_of(own_key, extent, shards, low, largest):
    def one(axis_at, shards_of):
        draws = jax.random.uniform(jax.random.fold_in(jax.random.fold_in(own_key, 6), axis_at), (shards_of,), jnp.float32, low / len(shards), largest / len(shards))
        return jnp.repeat(jnp.exp(draws), extent[axis_at] // shards_of).reshape((-1,) + (1,) * (len(extent) - axis_at - 1))

    factor_of = one(*shards[0])
    for cut in shards[1:]:
        factor_of = factor_of * one(*cut)
    return factor_of


def noise(rng, shape, deviation, bound, shards=(), held_as=jnp.bfloat16):
    values = jax.random.normal(rng, shape, jnp.float32) * deviation
    if len(shards) > 0:
        values = level_of(rng, shape, shards, -0.22, 0.18) * values
    return jnp.clip(values, min=-bound, max=bound).astype(held_as)


def setup_inputs(seed: int = 0) -> dict:
    streams_of = jax.random.split(jax.random.key(seed), 9)
    customer_inputs = noise(streams_of[0], (CUSTOMER_COUNT, F_IN), 1.0, 6.0, ((0, 32),))
    candidate_inputs = noise(streams_of[1], (CUSTOMER_COUNT, F_IN), 1.0, 6.0, ((0, 32),))
    affinity_sharpness = jnp.clip(jnp.exp(math.log(40.0) - 2.3025851 * jax.random.uniform(streams_of[2], (CUSTOMER_COUNT,), jnp.float32) ** level_of(streams_of[2], (CUSTOMER_COUNT,), ((0, 32),), -0.2, 0.2)), 4.0, 40.0).astype(jnp.bfloat16)
    correct_candidate_index = with_ends(jax.random.randint(streams_of[3], (CUSTOMER_COUNT,), 0, GROUP), jax.random.fold_in(streams_of[3], 1), 0, GROUP - 1).astype(jnp.int32)
    customer_initial_weights = noise(streams_of[4], (F_IN, HID), F_IN ** -0.5, 0.1875)
    customer_final_weights = noise(streams_of[5], (HID, EMB), HID ** -0.5, 0.25)
    candidate_initial_weights = noise(streams_of[6], (F_IN, HID), F_IN ** -0.5, 0.1875)
    candidate_final_weights = noise(streams_of[7], (HID, EMB), HID ** -0.5, 0.25)
    return dict(customer_inputs=customer_inputs, candidate_inputs=candidate_inputs, affinity_sharpness=affinity_sharpness, correct_candidate_index=correct_candidate_index, customer_initial_weights=customer_initial_weights, customer_final_weights=customer_final_weights, candidate_initial_weights=candidate_initial_weights, candidate_final_weights=candidate_final_weights)


EPS = 1e-06

def tower_forward(feats, first, second):
    pre = jnp.dot(feats, first, preferred_element_type=jnp.float32)
    hidden = jax.nn.relu(pre).astype(jnp.bfloat16)
    out = jnp.dot(hidden, second, preferred_element_type=jnp.float32)
    inv = lax.rsqrt(lax.optimization_barrier(jnp.mean(out * out, axis=-1, keepdims=True)) + EPS)
    return ((out * inv).astype(jnp.bfloat16), (pre, hidden, out, inv))

def tower_backward(feats, second, saved, grad_vec):
    pre, hidden, out, inv = saved
    grad = grad_vec.astype(jnp.float32)
    normed = out * inv
    grad_out = (inv * (grad - normed * lax.optimization_barrier(jnp.mean(grad * normed, axis=-1, keepdims=True)))).astype(jnp.bfloat16)
    grad_second = jnp.dot(hidden.T, grad_out, preferred_element_type=jnp.float32)
    grad_hidden = jnp.dot(grad_out, second.T, preferred_element_type=jnp.float32)
    grad_pre = jnp.where(pre > 0, grad_hidden, 0.0).astype(jnp.bfloat16)
    grad_first = jnp.dot(feats.T, grad_pre, preferred_element_type=jnp.float32)
    return (grad_first, grad_second)

def divide_among_cohorts(arr):
    rest = arr.shape[1:]
    split = arr.reshape((N_ROW, N_COL, MEMBERS_PER_CHIP) + rest)
    order = (1, 0, 2) + tuple(range(3, 3 + len(rest)))
    return split.transpose(order).reshape((N_COL, N_ROW * MEMBERS_PER_CHIP) + rest)

def from_groups(arr):
    rest = arr.shape[2:]
    split = arr.reshape((N_COL, N_ROW, MEMBERS_PER_CHIP) + rest)
    order = (1, 0, 2) + tuple(range(3, 3 + len(rest)))
    return split.transpose(order).reshape((N_ROW * N_COL * MEMBERS_PER_CHIP,) + rest)

def cohort_objective_values(args):
    shopper_vector, offered_thing_vector, sharpening_factor, pos = args
    latent_code = shopper_vector.shape[-1]
    coolness_fp32_number = sharpening_factor.astype(jnp.float32)
    affinity_matrix = coolness_fp32_number[:, None] * jnp.dot(shopper_vector, offered_thing_vector.T, preferred_element_type=jnp.float32) / latent_code
    lse = jax.nn.logsumexp(affinity_matrix, axis=1)
    columns = lax.broadcasted_iota(jnp.int32, affinity_matrix.shape, 1)
    target_column = columns == pos[:, None]
    picked = lax.optimization_barrier(jnp.sum(jnp.where(target_column, affinity_matrix, 0.0), axis=1))
    softmax_likelihood = jnp.exp(affinity_matrix - lse[:, None])
    sensitivity_of_affinities = ((softmax_likelihood - target_column.astype(jnp.float32)) * (coolness_fp32_number / (latent_code * MEMBERS_PER_CHIP))[:, None]).astype(jnp.bfloat16)
    customer_derivative = jnp.dot(sensitivity_of_affinities, offered_thing_vector, preferred_element_type=jnp.float32)
    candidate_derivative = jnp.dot(sensitivity_of_affinities.T, shopper_vector, preferred_element_type=jnp.float32)
    return (jnp.sum(lse - picked), customer_derivative, candidate_derivative)

def reference(customer_inputs, candidate_inputs, affinity_sharpness, correct_candidate_index, customer_initial_weights, customer_final_weights, candidate_initial_weights, candidate_final_weights):
    shopper_vector, user_saved = tower_forward(customer_inputs, customer_initial_weights, customer_final_weights)
    offered_thing_vector, item_saved = tower_forward(candidate_inputs, candidate_initial_weights, candidate_final_weights)
    running_accumulators, customer_derivative, candidate_derivative = lax.map(cohort_objective_values, (divide_among_cohorts(shopper_vector), divide_among_cohorts(offered_thing_vector), divide_among_cohorts(affinity_sharpness), divide_among_cohorts(correct_candidate_index)))
    loss = jnp.sum(running_accumulators) / customer_inputs.shape[0]
    grad_user_first, grad_user_second = tower_backward(customer_inputs, customer_final_weights, user_saved, from_groups(customer_derivative).astype(jnp.bfloat16))
    grad_item_first, grad_item_second = tower_backward(candidate_inputs, candidate_final_weights, item_saved, from_groups(candidate_derivative).astype(jnp.bfloat16))
    return (loss, grad_user_first, grad_user_second, grad_item_first, grad_item_second)
```

```python
import functools

import jax
import jax.numpy as jnp
from jax import lax
from jax.experimental import pallas as pl
from jax.experimental.pallas import tpu as pltpu
from jax.sharding import PartitionSpec as P

EPS = 1e-06
MESH = pl.DeviceIdType.MESH
F32 = jnp.float32
BF16 = jnp.bfloat16
TILE = 256


def mm(a, b, ca=1, cb=0):
    return lax.dot_general(a, b, (((ca,), (cb,)), ((), ())), preferred_element_type=F32)


def kernel(
    R, C, T, M, F, H, E, hold,
    xu_hbm, xi_hbm, sharp_ref, pos_ref, w1u_hbm, w2u_hbm, w1i_hbm, w2i_hbm,
    fin_hbm, loss_ref,
    X, W1, W2, HID, OUT, U, IT, EX, D, GI, RR, RL, GU, GV, GP, LS, PK,
    B, P1, P2, S2, P3, FIN, L0, L1, L2, L3,
    in_sem, out_sem, ag_send, ag_recv, rs_send, rs_recv,
    c1s, c1r, c2s, c2r, c3s, c3r, c4s, c4r, c5s, c5r, c6s, c6r, ls, lr,
):
    C2 = C // 2
    r = lax.axis_index("row")
    c = lax.axis_index("col")
    core = lax.rem(c, 2)
    chip = c // 2
    partner = chip * 2 + (1 - core)
    NH = C2 * R * T
    NT = 2 * NH
    RT = R * T
    loads = []
    for t, (xh, w1h, w2h) in enumerate(((xi_hbm, w1i_hbm, w2i_hbm), (xu_hbm, w1u_hbm, w2u_hbm))):
        for k, (src, dst) in enumerate(((w1h, W1.at[t]), (w2h, W2.at[t]), (xh, X.at[t]))):
            loads.append(pltpu.make_async_copy(src, dst, in_sem.at[t, k]))
    for cp in loads:
        cp.start()

    barrier = pltpu.get_barrier_semaphore()
    for j in range(1, R):
        pl.semaphore_signal(barrier, inc=1, device_id=(lax.rem(r + j, R), c), device_id_type=MESH)
    for j in range(1, C2):
        pl.semaphore_signal(
            barrier, inc=1, device_id=(r, lax.rem(chip + j, C2) * 2 + core), device_id_type=MESH
        )
    pl.semaphore_signal(barrier, inc=1, device_id=(r, partner), device_id_type=MESH)

    def rows(i):
        return pl.ds(pl.multiple_of(i * TILE, TILE), TILE)

    def forward(t, put):
        def step(i, _):
            s = rows(i)
            pre = mm(X[t, s, :], W1[t])
            h = jnp.maximum(pre, 0.0).astype(BF16)
            HID[t, s, :] = h
            out = mm(h, W2[t])
            OUT[t, s, :] = out
            inv = lax.rsqrt(jnp.mean(out * out, axis=-1, keepdims=True) + EPS)
            put(s, (out * inv).astype(BF16))
            return 0

        lax.fori_loop(0, M // TILE, step, 0)

    for cp in loads[:3]:
        cp.wait()

    def put_item(s, v):
        IT[r, s, :] = v

    forward(0, put_item)
    pl.semaphore_wait(barrier, R + C2 - 1)

    def ag(b, right):
        d = 1 if right else 0
        return pltpu.make_async_remote_copy(
            src_ref=IT.at[b], dst_ref=IT.at[b], send_sem=ag_send.at[d, b], recv_sem=ag_recv.at[b],
            device_id=(r + 1 if right else r - 1, c), device_id_type=MESH,
        )

    @pl.when(r < R - 1)
    def _():
        ag(r, True).start()

    @pl.when(r > 0)
    def _():
        ag(r, False).start()

    for cp in loads[3:]:
        cp.wait()

    def put_user(s, v):
        U[s, :] = v

    forward(1, put_user)
    LS[...] = jnp.zeros_like(LS)
    PK[...] = jnp.zeros_like(PK)
    factor = sharp_ref[...].astype(F32) * (1.0 / E)
    positive = pos_ref[...]

    def score(b):
        def step(i, _):
            s = rows(i)
            logit = mm(IT[b, s, :], U[...], 1, 1) * factor
            item = lax.broadcasted_iota(jnp.int32, logit.shape, 0) + (b * M + i * TILE)
            e = jnp.exp(logit)
            if hold:
                EX[b, s, :] = e
            LS[...] += jnp.sum(e, axis=0, keepdims=True)
            PK[...] += jnp.sum(jnp.where(item == positive, logit, 0.0), axis=0, keepdims=True)
            return 0

        lax.fori_loop(0, M // TILE, step, 0)

    score(r)

    def arrive(d, _):
        lo = r - d
        hi = r + d

        @pl.when(lo >= 0)
        def _():
            ag(lo, True).wait_recv()

            @pl.when(r < R - 1)
            def _():
                ag(lo, True).start()

        @pl.when(hi < R)
        def _():
            ag(hi, False).wait_recv()

            @pl.when(r > 0)
            def _():
                ag(hi, False).start()

        def one(k, _):
            b = lo + k * (hi - lo)

            @pl.when(jnp.logical_and(b >= 0, b < R))
            def _():
                score(b)

            return 0

        lax.fori_loop(0, 2, one, 0)
        return 0

    lax.fori_loop(1, R, arrive, 0)

    L0[...] = jnp.full(L0.shape, jnp.sum(jnp.log(LS[...]) - PK[...]), F32)
    GU[...] = jnp.zeros_like(GU)
    rate = factor * (1.0 / M)
    norm = 1.0 / LS[...]

    def back(b):
        def step(i, _):
            s = rows(i)
            item = lax.broadcasted_iota(jnp.int32, (TILE, M), 0) + (b * M + i * TILE)
            hit = jnp.where(item == positive, 1.0, 0.0)
            e = EX[b, s, :] if hold else jnp.exp(mm(IT[b, s, :], U[...], 1, 1) * factor)
            d = ((e * norm - hit) * rate).astype(BF16)
            D[b, s, :] = d
            GI[b, s, :] = mm(d, U[...]).astype(BF16)
            return 0

        lax.fori_loop(0, M // TILE, step, 0)

    def rs(b, right):
        d = 1 if right else 0
        land = RR if right else RL
        return pltpu.make_async_remote_copy(
            src_ref=GI.at[b], dst_ref=land.at[b], send_sem=rs_send.at[b], recv_sem=rs_recv.at[d, b],
            device_id=(r + 1 if right else r - 1, c), device_id_type=MESH,
        )

    def leave(k, _):
        d = R - 1 - k
        lo = r - d
        hi = r + d

        def one(q, _):
            b = hi + q * (lo - hi)

            @pl.when(jnp.logical_and(b >= 0, b < R))
            def _():
                back(b)

            return 0

        lax.fori_loop(0, 2, one, 0)

        @pl.when(jnp.logical_and(hi < R, r == 0))
        def _():
            rs(hi, True).start()

        @pl.when(jnp.logical_and(lo >= 0, r == R - 1))
        def _():
            rs(lo, False).start()

        return 0

    lax.fori_loop(0, R - 1, leave, 0)

    def add_rows(dst, b, land):
        def step(i, _):
            s = rows(i)
            dst[b, s, :] = (dst[b, s, :].astype(F32) + land[b, s, :].astype(F32)).astype(BF16)
            return 0

        lax.fori_loop(0, M // TILE, step, 0)

    def relay(k):
        hi = R - 1 - k
        lo = k

        @pl.when(jnp.logical_and(hi > r, r > 0))
        def _():
            rs(hi, True).wait_recv()
            add_rows(GI, hi, RR)
            rs(hi, True).start()

        @pl.when(jnp.logical_and(lo < r, r < R - 1))
        def _():
            rs(lo, False).wait_recv()
            add_rows(GI, lo, RL)
            rs(lo, False).start()

    back(r)

    def user_grad(b, _):
        def step(i, _):
            s = rows(i)
            GU[s, :] += mm(D[b, :, s], IT[b], 0, 0)
            return 0

        lax.fori_loop(0, M // TILE, step, 0)
        return 0

    def backward_in(t, grad):
        def step(i, _):
            s = rows(i)
            g = grad(s)
            out = OUT[t, s, :]
            inv = lax.rsqrt(jnp.mean(out * out, axis=-1, keepdims=True) + EPS)
            n = out * inv
            go = (inv * (g - n * jnp.mean(g * n, axis=-1, keepdims=True))).astype(BF16)
            GV[s, :] = go
            gh = mm(go, W2[t], 1, 1)
            GP[s, :] = jnp.where(HID[t, s, :].astype(F32) > 0, gh, 0.0).astype(BF16)
            return 0

        lax.fori_loop(0, M // TILE, step, 0)

    def lay(t, base, height, i, v):
        for k in range(v.shape[1] // 128):
            part = v[:, k * 128 : (k + 1) * 128].astype(BF16).reshape(TILE // 16, 16, 128)
            B[t, pl.ds(base + k * (height // 16) + i * (TILE // 16), TILE // 16)] = part

    def backward_out(t):
        def second(i, _):
            lay(t, (F // 16) * (H // 128), H, i, mm(HID[t, :, rows(i)], GV[...], 0, 0))
            return 0

        lax.fori_loop(0, H // TILE, second, 0)

        def first(i, _):
            lay(t, 0, F, i, mm(X[t, :, rows(i)], GP[...], 0, 0))
            return 0

        lax.fori_loop(0, F // TILE, first, 0)

    def remote(src, dst, ss, rr, dev):
        return pltpu.make_async_remote_copy(
            src_ref=src, dst_ref=dst, send_sem=ss, recv_sem=rr, device_id=dev, device_id_type=MESH
        )

    half = core * NH
    mine = half + chip * RT
    tile0 = mine + r * T

    def cp1(t):
        return [remote(B.at[t, pl.ds((1 - core) * NH, NH)], P1.at[t], c1s.at[t], c1r.at[t], (r, partner))]

    def cp2(t):
        out = []
        for j in range(1, C2):
            to = lax.rem(chip + j, C2)
            out.append(remote(B.at[t, pl.ds(half + to * RT, RT)], P2.at[t, j - 1], c2s.at[t, j - 1],
                              c2r.at[t, j - 1], (r, to * 2 + core)))
        return out

    def cp3(t):
        out = []
        for j in range(1, R):
            to = lax.rem(r + j, R)
            out.append(remote(S2.at[t, pl.ds(to * T, T)], P3.at[t, j - 1], c3s.at[t, j - 1],
                              c3r.at[t, j - 1], (to, c)))
        return out

    def cp4(t):
        ref = FIN.at[t, pl.ds(tile0, T)]
        return [remote(ref, ref, c4s.at[t, j - 1], c4r.at[t, j - 1], (lax.rem(r + j, R), c))
                for j in range(1, R)]

    def cp4_in(t):
        out = []
        for j in range(1, R):
            ref = FIN.at[t, pl.ds(mine + lax.rem(r + R - j, R) * T, T)]
            out.append(remote(ref, ref, c4s.at[t, j - 1], c4r.at[t, j - 1], (lax.rem(r + j, R), c)))
        return out

    def cp5(t):
        ref = FIN.at[t, pl.ds(mine, RT)]
        return [remote(ref, ref, c5s.at[t, j - 1], c5r.at[t, j - 1],
                       (r, lax.rem(chip + j, C2) * 2 + core)) for j in range(1, C2)]

    def cp5_in(t):
        out = []
        for j in range(1, C2):
            ref = FIN.at[t, pl.ds(half + lax.rem(chip + C2 - j, C2) * RT, RT)]
            out.append(remote(ref, ref, c5s.at[t, j - 1], c5r.at[t, j - 1],
                              (r, lax.rem(chip + j, C2) * 2 + core)))
        return out

    def cp6(t):
        ref = FIN.at[t, pl.ds(half, NH)]
        return [remote(ref, ref, c6s.at[t], c6r.at[t], (r, partner))]

    def cp6_in(t):
        ref = FIN.at[t, pl.ds((1 - core) * NH, NH)]
        return [remote(ref, ref, c6s.at[t], c6r.at[t], (r, partner))]

    def start(cps):
        for cp in cps:
            cp.start()

    def arrived(cps):
        for cp in cps:
            cp.wait_recv()

    def sum1(t):
        arrived(cp1(t))

        def step(i, _):
            at = pl.ds(half + i * RT, RT)
            B[t, at] = (B[t, at].astype(F32) + P1[t, pl.ds(i * RT, RT)].astype(F32)).astype(BF16)
            return 0

        lax.fori_loop(0, C2, step, 0)
        start(cp2(t))

    def sum2(t):
        arrived(cp2(t))
        total = B[t, pl.ds(mine, RT)].astype(F32)
        for j in range(C2 - 1):
            total += P2[t, j].astype(F32)
        S2[t] = total.astype(BF16)
        start(cp3(t))

    def sum3(t):
        arrived(cp3(t))
        total = S2[t, pl.ds(r * T, T)].astype(F32)
        for j in range(R - 1):
            total += P3[t, j].astype(F32)
        FIN[t, pl.ds(tile0, T)] = total.astype(BF16)
        start(cp4(t))

    def share5(t):
        arrived(cp4_in(t))
        start(cp5(t))

    def share6(t):
        arrived(cp5_in(t))
        start(cp6(t))

    def finish(t):
        arrived(cp6_in(t))
        return pltpu.make_async_copy(FIN.at[t], fin_hbm.at[t], out_sem.at[t])

    loss1 = [remote(L0, L1, ls.at[0], lr.at[0], (r, partner))]
    loss2 = [remote(L2.at[0], L2.at[j], ls.at[j], lr.at[j], (r, lax.rem(chip + j, C2) * 2 + core))
             for j in range(1, C2)]
    loss3 = [remote(L3.at[0], L3.at[j], ls.at[C2 - 1 + j], lr.at[C2 - 1 + j], (lax.rem(r + j, R), c))
             for j in range(1, R)]

    start(loss1)
    relay(0)
    lax.fori_loop(0, R, user_grad, 0)
    if R > 2:
        relay(1)
    backward_in(1, lambda s: GU[s, :].astype(BF16).astype(F32))
    if R > 3:
        relay(2)
    backward_out(1)
    start(cp1(1))
    for k in range(3, R - 1):
        relay(k)
    arrived(loss1)
    L2[0] = L0[...] + L1[...]
    start(loss2)

    @pl.when(r > 0)
    def _():
        rs(r, True).wait_recv()

    sum1(1)

    @pl.when(r < R - 1)
    def _():
        rs(r, False).wait_recv()

    has_left = jnp.where(r > 0, 1.0, 0.0)
    has_right = jnp.where(r < R - 1, 1.0, 0.0)

    @pl.when(r > 0)
    def _():
        add_rows(GI, r, RR)

    @pl.when(r < R - 1)
    def _():
        add_rows(GI, r, RL)

    backward_in(0, lambda s: GI[r, s, :].astype(F32))
    sum2(1)
    backward_out(0)
    start(cp1(0))
    arrived(loss2)
    L3[0] = functools.reduce(lambda a, b: a + b, [L2[j] for j in range(C2)])
    start(loss3)
    sum3(1)
    sum1(0)
    share5(1)
    sum2(0)
    share6(1)
    sum3(0)
    out1 = finish(1)
    out1.start()
    share5(0)
    arrived(loss3)
    loss_ref[...] = functools.reduce(lambda a, b: a + b, [L3[j] for j in range(R)])
    share6(0)
    out0 = finish(0)
    out0.start()

    def sent(b, _):
        @pl.when(jnp.logical_and(r < R - 1, b <= r))
        def _():
            ag(b, True).wait_send()

        @pl.when(jnp.logical_and(r > 0, b >= r))
        def _():
            ag(b, False).wait_send()

        @pl.when(b > r)
        def _():
            rs(b, True).wait_send()

        @pl.when(b < r)
        def _():
            rs(b, False).wait_send()

        return 0

    lax.fori_loop(0, R, sent, 0)
    for t in range(2):
        for cps in (cp1(t), cp2(t), cp3(t), cp4(t), cp5(t), cp6(t)):
            for cp in cps:
                cp.wait_send()
    for cp in loss1 + loss2 + loss3:
        cp.wait_send()
    out1.wait()
    out0.wait()


def solution(mesh):
    R, C = mesh.shape["row"], mesh.shape["col"]
    C2 = C // 2

    def body(xu, xi, sharp, pos, w1u, w2u, w1i, w2i):
        M, F = xu.shape
        H, E = w2u.shape
        tiles = (F // 16) * (H // 128) + (H // 16) * (E // 128)
        T = -(-tiles // (R * C))
        NT = T * R * C
        RT = R * T
        hold = R * M * M * 4 <= 1 << 24
        V = pltpu.VMEM
        DMA = pltpu.SemaphoreType.DMA
        hbm = pl.BlockSpec(memory_space=pl.ANY)
        vmem = pl.BlockSpec(memory_space=pltpu.VMEM)
        fin, loss = pl.pallas_call(
            functools.partial(kernel, R, C, T, M, F, H, E, hold),
            name="step",
            out_shape=(
                jax.ShapeDtypeStruct((2, NT, 16, 128), BF16),
                jax.ShapeDtypeStruct((8, 128), F32),
            ),
            in_specs=[hbm, hbm, vmem, vmem, hbm, hbm, hbm, hbm],
            out_specs=(hbm, vmem),
            scratch_shapes=[
                V((2, M, F), BF16), V((2, F, H), BF16), V((2, H, E), BF16),
                V((2, M, H), BF16), V((2, M, E), F32), V((M, E), BF16),
                V((R, M, E), BF16), V((R, M, M) if hold else (1, 8, 128), F32), V((R, M, M), BF16),
                V((R, M, E), BF16), V((R, M, E), BF16), V((R, M, E), BF16),
                V((M, E), F32), V((M, E), BF16), V((M, H), BF16),
                V((1, M), F32), V((1, M), F32),
                V((2, NT, 16, 128), BF16), V((2, NT // 2, 16, 128), BF16),
                V((2, C2 - 1, RT, 16, 128), BF16), V((2, RT, 16, 128), BF16),
                V((2, R - 1, T, 16, 128), BF16), V((2, NT, 16, 128), BF16),
                V((8, 128), F32), V((8, 128), F32), V((C2, 8, 128), F32), V((R, 8, 128), F32),
                DMA((2, 3)), DMA((2,)), DMA((2, R)), DMA((R,)), DMA((R,)), DMA((2, R)),
                DMA((2,)), DMA((2,)), DMA((2, C2 - 1)), DMA((2, C2 - 1)),
                DMA((2, R - 1)), DMA((2, R - 1)), DMA((2, R - 1)), DMA((2, R - 1)),
                DMA((2, C2 - 1)), DMA((2, C2 - 1)), DMA((2,)), DMA((2,)),
                DMA((C2 + R,)), DMA((C2 + R,)),
            ],
            compiler_params=pltpu.CompilerParams(
                collective_id=0, has_side_effects=True, vmem_limit_bytes=67043328
            ),
        )(xu, xi, sharp[None, :], pos[None, :], w1u, w2u, w1i, w2i)

        def unpack(t):
            flat = fin[t].reshape(NT * 16, 128)
            n1 = F * (H // 128)
            n2 = H * (E // 128)
            first = flat[:n1].reshape(H // 128, F, 128).transpose(1, 0, 2).reshape(F, H)
            second = flat[n1 : n1 + n2].reshape(E // 128, H, 128).transpose(1, 0, 2).reshape(H, E)
            return first.astype(F32), second.astype(F32)

        i1, i2 = unpack(0)
        u1, u2 = unpack(1)
        return (loss[0, 0] / (M * R * C), u1, u2, i1, i2)

    placed = (
        P(("row", "col"), None), P(("row", "col"), None), P(("row", "col")), P(("row", "col")),
        P(), P(), P(), P(),
    )
    return jax.shard_map(
        body, mesh=mesh, in_specs=placed, out_specs=(P(), P(), P(), P(), P()), check_vma=False
    )
```

```python
import functools

import jax
import jax.numpy as jnp
from jax import lax
from jax.experimental import pallas as pl
from jax.experimental.pallas import tpu as pltpu
from jax.sharding import PartitionSpec as P

EPS = 1e-06
MESH = pl.DeviceIdType.MESH
F32 = jnp.float32
BF16 = jnp.bfloat16
TILE = 256


def mm(a, b, ca=1, cb=0):
    return lax.dot_general(a, b, (((ca,), (cb,)), ((), ())), preferred_element_type=F32)


def kernel(
    R, C, T, M, F, H, E, hold,
    xu_hbm, xi_hbm, sharp_ref, pos_ref, w1u_hbm, w2u_hbm, w1i_hbm, w2i_hbm,
    fin_hbm, loss_ref,
    X, W1, W2, HID, OUT, U, IT, EX, D, GI, RR, RL, GU, GV, GP, LS, PK,
    B, P1, P2, S2, P3, FIN, L0, L1, L2, L3, FS, PS, SUMS, OTHER,
    in_sem, out_sem, ag_send, ag_recv, rs_send, rs_recv,
    c1s, c1r, c2s, c2r, c3s, c3r, c4s, c4r, c5s, c5r, c6s, c6r, ls, lr, sq_send, sq_recv,
):
    C2 = C // 2
    square = R == 4 and hold
    r = lax.axis_index("row")
    c = lax.axis_index("col")
    core = lax.rem(c, 2)
    chip = c // 2
    partner = chip * 2 + (1 - core)
    NH = C2 * R * T
    NT = 2 * NH
    RT = R * T
    loads = []
    for t, (xh, w1h, w2h) in enumerate(((xi_hbm, w1i_hbm, w2i_hbm), (xu_hbm, w1u_hbm, w2u_hbm))):
        for k, (src, dst) in enumerate(((w1h, W1.at[t]), (w2h, W2.at[t]), (xh, X.at[t]))):
            loads.append(pltpu.make_async_copy(src, dst, in_sem.at[t, k]))
    for cp in loads:
        cp.start()

    barrier = pltpu.get_barrier_semaphore()
    for j in range(1, R):
        pl.semaphore_signal(barrier, inc=1, device_id=(lax.rem(r + j, R), c), device_id_type=MESH)
    for j in range(1, C2):
        pl.semaphore_signal(
            barrier, inc=1, device_id=(r, lax.rem(chip + j, C2) * 2 + core), device_id_type=MESH
        )
    pl.semaphore_signal(barrier, inc=1, device_id=(r, partner), device_id_type=MESH)

    def rows(i):
        return pl.ds(pl.multiple_of(i * TILE, TILE), TILE)

    def forward(t, put):
        def step(i, _):
            s = rows(i)
            pre = mm(X[t, s, :], W1[t])
            h = jnp.maximum(pre, 0.0).astype(BF16)
            HID[t, s, :] = h
            out = mm(h, W2[t])
            OUT[t, s, :] = out
            inv = lax.rsqrt(jnp.mean(out * out, axis=-1, keepdims=True) + EPS)
            put(s, (out * inv).astype(BF16))
            return 0

        lax.fori_loop(0, M // TILE, step, 0)

    for cp in loads[:3]:
        cp.wait()

    def put_item(s, v):
        IT[0 if square else r, s, :] = v

    forward(0, put_item)
    pl.semaphore_wait(barrier, R + C2 - 1)

    if square:
        inner = jnp.logical_or(r == 1, r == 2)
        outer = jnp.logical_not(inner)
        side = r // 2
        buddy = side * 2 + (1 - lax.rem(r, 2))
        across = 2 - side
        beyond = 3 - 3 * side
        first_slot = jnp.where(inner, 1, 0)

        def block_of(slot):
            near = jnp.where(inner, across, buddy)
            return jnp.where(slot == 0, r, jnp.where(slot == 1, near, beyond))

        def to(src, dst, k, row, ks=None):
            return pltpu.make_async_remote_copy(
                src_ref=src, dst_ref=dst, send_sem=sq_send.at[k if ks is None else ks], recv_sem=sq_recv.at[k],
                device_id=(row, c), device_id_type=MESH,
            )

        item_near = to(IT.at[0], IT.at[1], 0, across)
        item_buddy = to(IT.at[0], IT.at[1], 1, buddy)
        item_far = to(IT.at[0], IT.at[2], 2, across)
        user_out = to(U.at[0], U.at[1], 3, buddy)
        scale_out = to(FS.at[0], FS.at[1], 4, buddy)
        place_out = to(PS.at[0], PS.at[1], 5, buddy)

        @pl.when(inner)
        def _():
            item_near.start()
            item_buddy.start()

        @pl.when(outer)
        def _():
            item_far.start()

        FS[0] = sharp_ref[...].astype(F32) * (1.0 / E)
        PS[0] = pos_ref[...]
        for cp in loads[3:]:
            cp.wait()

        def put_user(s, v):
            U[0, s, :] = v

        forward(1, put_user)
        user_out.start()
        scale_out.start()
        place_out.start()
        SUMS[...] = jnp.zeros_like(SUMS)

        def score(q, slot):
            b = block_of(slot)
            pair = q * 2 + slot - first_slot
            factor = FS[q]
            positive = PS[q]

            def step(i, _):
                s = rows(i)
                logit = mm(IT[slot, s, :], U[q], 1, 1) * factor
                item = lax.broadcasted_iota(jnp.int32, logit.shape, 0) + (b * M + i * TILE)
                e = jnp.exp(logit)
                EX[pair, s, :] = e
                SUMS[q] += jnp.sum(e, axis=0, keepdims=True)
                SUMS[2 + q] += jnp.sum(
                    jnp.where(item == positive, logit, 0.0), axis=0, keepdims=True
                )
                return 0

            lax.fori_loop(0, M // TILE, step, 0)

        @pl.when(outer)
        def _():
            score(0, 0)
            item_buddy.wait_recv()

        @pl.when(inner)
        def _():
            item_near.wait_recv()

        score(0, 1)
        scale_out.wait_recv()
        place_out.wait_recv()
        user_out.wait_recv()
        score(1, 1)

        @pl.when(outer)
        def _():
            score(1, 0)

        @pl.when(inner)
        def _():
            item_far.wait_recv()

            def both(q, _):
                score(q, 2)
                return 0

            lax.fori_loop(0, 2, both, 0)

        swap = to(SUMS, OTHER, 6, buddy)
        swap.start()
        swap.wait_recv()
        total0 = SUMS[0] + OTHER[1]
        total1 = SUMS[1] + OTHER[0]
        L0[...] = jnp.full(L0.shape, jnp.sum(jnp.log(total0) - (SUMS[2] + OTHER[3])), F32)
        NORM = (1.0 / total0, 1.0 / total1)

        def back(q, k):
            b = block_of(first_slot + k)
            rate = FS[q] * (1.0 / M)
            positive = PS[q]

            def step(i, _):
                s = rows(i)
                item = lax.broadcasted_iota(jnp.int32, (TILE, M), 0) + (b * M + i * TILE)
                hit = jnp.where(item == positive, 1.0, 0.0)
                D[2 * q + k, s, :] = ((EX[2 * q + k, s, :] * NORM[q] - hit) * rate).astype(BF16)
                return 0

            lax.fori_loop(0, M // TILE, step, 0)

        def user_part(q, put):
            def step(i, _):
                s = rows(i)
                put(s, mm(D[2 * q, :, s], IT[first_slot], 0, 0)
                    + mm(D[2 * q + 1, :, s], IT[first_slot + 1], 0, 0))
                return 0

            lax.fori_loop(0, M // TILE, step, 0)

        def put_sent(s, v):
            RL[0, s, :] = v.astype(BF16)

        def put_kept(s, v):
            GU[0, s, :] = v

        user_home = to(RL.at[0], RL.at[1], 7, buddy)
        back(1, 0)
        back(1, 1)
        user_part(1, put_sent)
        user_home.start()
        back(0, 0)
        back(0, 1)

        def item_part(k):
            def step(i, _):
                s = rows(i)
                GI[k, s, :] = (mm(D[k, s, :], U[0]) + mm(D[2 + k, s, :], U[1])).astype(BF16)
                return 0

            lax.fori_loop(0, M // TILE, step, 0)

        far_home = to(GI.at[1], RR.at[0], 8, beyond, 10)
        near_home = to(GI.at[0], RR.at[0], 8, across)
        buddy_home = to(GI.at[1], RR.at[1], 9, buddy)
        item_part(1)

        @pl.when(inner)
        def _():
            far_home.start()

        @pl.when(outer)
        def _():
            buddy_home.start()

        item_part(0)

        @pl.when(inner)
        def _():
            near_home.start()

        @pl.when(outer)
        def _():
            RR[1] = GI[0]

    else:

        def ag(b, right):
            d = 1 if right else 0
            return pltpu.make_async_remote_copy(
                src_ref=IT.at[b], dst_ref=IT.at[b], send_sem=ag_send.at[d, b], recv_sem=ag_recv.at[b],
                device_id=(r + 1 if right else r - 1, c), device_id_type=MESH,
            )

        @pl.when(r < R - 1)
        def _():
            ag(r, True).start()

        @pl.when(r > 0)
        def _():
            ag(r, False).start()

        for cp in loads[3:]:
            cp.wait()

        def put_user(s, v):
            U[0, s, :] = v

        forward(1, put_user)
        LS[...] = jnp.zeros_like(LS)
        PK[...] = jnp.zeros_like(PK)
        factor = sharp_ref[...].astype(F32) * (1.0 / E)
        positive = pos_ref[...]

        def score(b):
            def step(i, _):
                s = rows(i)
                logit = mm(IT[b, s, :], U[0], 1, 1) * factor
                item = lax.broadcasted_iota(jnp.int32, logit.shape, 0) + (b * M + i * TILE)
                e = jnp.exp(logit)
                if hold:
                    EX[b, s, :] = e
                LS[...] += jnp.sum(e, axis=0, keepdims=True)
                PK[...] += jnp.sum(jnp.where(item == positive, logit, 0.0), axis=0, keepdims=True)
                return 0

            lax.fori_loop(0, M // TILE, step, 0)

        score(r)

        def arrive(d, _):
            lo = r - d
            hi = r + d

            @pl.when(lo >= 0)
            def _():
                ag(lo, True).wait_recv()

                @pl.when(r < R - 1)
                def _():
                    ag(lo, True).start()

            @pl.when(hi < R)
            def _():
                ag(hi, False).wait_recv()

                @pl.when(r > 0)
                def _():
                    ag(hi, False).start()

            def one(k, _):
                b = lo + k * (hi - lo)

                @pl.when(jnp.logical_and(b >= 0, b < R))
                def _():
                    score(b)

                return 0

            lax.fori_loop(0, 2, one, 0)
            return 0

        lax.fori_loop(1, R, arrive, 0)

        L0[...] = jnp.full(L0.shape, jnp.sum(jnp.log(LS[...]) - PK[...]), F32)
        GU[0] = jnp.zeros((M, E), F32)
        rate = factor * (1.0 / M)
        norm = 1.0 / LS[...]

        def back(b):
            def step(i, _):
                s = rows(i)
                item = lax.broadcasted_iota(jnp.int32, (TILE, M), 0) + (b * M + i * TILE)
                hit = jnp.where(item == positive, 1.0, 0.0)
                e = EX[b, s, :] if hold else jnp.exp(mm(IT[b, s, :], U[0], 1, 1) * factor)
                d = ((e * norm - hit) * rate).astype(BF16)
                D[b, s, :] = d
                GI[b, s, :] = mm(d, U[0]).astype(BF16)
                return 0

            lax.fori_loop(0, M // TILE, step, 0)

        def rs(b, right):
            d = 1 if right else 0
            land = RR if right else RL
            return pltpu.make_async_remote_copy(
                src_ref=GI.at[b], dst_ref=land.at[b], send_sem=rs_send.at[b], recv_sem=rs_recv.at[d, b],
                device_id=(r + 1 if right else r - 1, c), device_id_type=MESH,
            )

        def leave(k, _):
            d = R - 1 - k
            lo = r - d
            hi = r + d

            def one(q, _):
                b = hi + q * (lo - hi)

                @pl.when(jnp.logical_and(b >= 0, b < R))
                def _():
                    back(b)

                return 0

            lax.fori_loop(0, 2, one, 0)

            @pl.when(jnp.logical_and(hi < R, r == 0))
            def _():
                rs(hi, True).start()

            @pl.when(jnp.logical_and(lo >= 0, r == R - 1))
            def _():
                rs(lo, False).start()

            return 0

        lax.fori_loop(0, R - 1, leave, 0)

        def add_rows(dst, b, land):
            def step(i, _):
                s = rows(i)
                dst[b, s, :] = (dst[b, s, :].astype(F32) + land[b, s, :].astype(F32)).astype(BF16)
                return 0

            lax.fori_loop(0, M // TILE, step, 0)

        def relay(k):
            hi = R - 1 - k
            lo = k

            @pl.when(jnp.logical_and(hi > r, r > 0))
            def _():
                rs(hi, True).wait_recv()
                add_rows(GI, hi, RR)
                rs(hi, True).start()

            @pl.when(jnp.logical_and(lo < r, r < R - 1))
            def _():
                rs(lo, False).wait_recv()
                add_rows(GI, lo, RL)
                rs(lo, False).start()

        back(r)

        def user_grad(b, _):
            def step(i, _):
                s = rows(i)
                GU[0, s, :] += mm(D[b, :, s], IT[b], 0, 0)
                return 0

            lax.fori_loop(0, M // TILE, step, 0)
            return 0

    def backward_in(t, grad):
        def step(i, _):
            s = rows(i)
            g = grad(s)
            out = OUT[t, s, :]
            inv = lax.rsqrt(jnp.mean(out * out, axis=-1, keepdims=True) + EPS)
            n = out * inv
            go = (inv * (g - n * jnp.mean(g * n, axis=-1, keepdims=True))).astype(BF16)
            GV[s, :] = go
            gh = mm(go, W2[t], 1, 1)
            GP[s, :] = jnp.where(HID[t, s, :].astype(F32) > 0, gh, 0.0).astype(BF16)
            return 0

        lax.fori_loop(0, M // TILE, step, 0)

    def lay(t, base, height, i, v):
        for k in range(v.shape[1] // 128):
            part = v[:, k * 128 : (k + 1) * 128].astype(BF16).reshape(TILE // 16, 16, 128)
            B[t, pl.ds(base + k * (height // 16) + i * (TILE // 16), TILE // 16)] = part

    def backward_out(t):
        def second(i, _):
            lay(t, (F // 16) * (H // 128), H, i, mm(HID[t, :, rows(i)], GV[...], 0, 0))
            return 0

        lax.fori_loop(0, H // TILE, second, 0)

        def first(i, _):
            lay(t, 0, F, i, mm(X[t, :, rows(i)], GP[...], 0, 0))
            return 0

        lax.fori_loop(0, F // TILE, first, 0)

    def remote(src, dst, ss, rr, dev):
        return pltpu.make_async_remote_copy(
            src_ref=src, dst_ref=dst, send_sem=ss, recv_sem=rr, device_id=dev, device_id_type=MESH
        )

    half = core * NH
    mine = half + chip * RT
    tile0 = mine + r * T

    def cp1(t):
        return [remote(B.at[t, pl.ds((1 - core) * NH, NH)], P1.at[t], c1s.at[t], c1r.at[t], (r, partner))]

    def cp2(t):
        out = []
        for j in range(1, C2):
            to = lax.rem(chip + j, C2)
            out.append(remote(B.at[t, pl.ds(half + to * RT, RT)], P2.at[t, j - 1], c2s.at[t, j - 1],
                              c2r.at[t, j - 1], (r, to * 2 + core)))
        return out

    def cp3(t):
        out = []
        for j in range(1, R):
            to = lax.rem(r + j, R)
            out.append(remote(S2.at[t, pl.ds(to * T, T)], P3.at[t, j - 1], c3s.at[t, j - 1],
                              c3r.at[t, j - 1], (to, c)))
        return out

    def cp4(t):
        ref = FIN.at[t, pl.ds(tile0, T)]
        return [remote(ref, ref, c4s.at[t, j - 1], c4r.at[t, j - 1], (lax.rem(r + j, R), c))
                for j in range(1, R)]

    def cp4_in(t):
        out = []
        for j in range(1, R):
            ref = FIN.at[t, pl.ds(mine + lax.rem(r + R - j, R) * T, T)]
            out.append(remote(ref, ref, c4s.at[t, j - 1], c4r.at[t, j - 1], (lax.rem(r + j, R), c)))
        return out

    def cp5(t):
        ref = FIN.at[t, pl.ds(mine, RT)]
        return [remote(ref, ref, c5s.at[t, j - 1], c5r.at[t, j - 1],
                       (r, lax.rem(chip + j, C2) * 2 + core)) for j in range(1, C2)]

    def cp5_in(t):
        out = []
        for j in range(1, C2):
            ref = FIN.at[t, pl.ds(half + lax.rem(chip + C2 - j, C2) * RT, RT)]
            out.append(remote(ref, ref, c5s.at[t, j - 1], c5r.at[t, j - 1],
                              (r, lax.rem(chip + j, C2) * 2 + core)))
        return out

    def cp6(t):
        ref = FIN.at[t, pl.ds(half, NH)]
        return [remote(ref, ref, c6s.at[t], c6r.at[t], (r, partner))]

    def cp6_in(t):
        ref = FIN.at[t, pl.ds((1 - core) * NH, NH)]
        return [remote(ref, ref, c6s.at[t], c6r.at[t], (r, partner))]

    def start(cps):
        for cp in cps:
            cp.start()

    def arrived(cps):
        for cp in cps:
            cp.wait_recv()

    def sum1(t):
        arrived(cp1(t))

        def step(i, _):
            at = pl.ds(half + i * RT, RT)
            B[t, at] = (B[t, at].astype(F32) + P1[t, pl.ds(i * RT, RT)].astype(F32)).astype(BF16)
            return 0

        lax.fori_loop(0, C2, step, 0)
        start(cp2(t))

    def sum2(t):
        arrived(cp2(t))
        total = B[t, pl.ds(mine, RT)].astype(F32)
        for j in range(C2 - 1):
            total += P2[t, j].astype(F32)
        S2[t] = total.astype(BF16)
        start(cp3(t))

    def sum3(t):
        arrived(cp3(t))
        total = S2[t, pl.ds(r * T, T)].astype(F32)
        for j in range(R - 1):
            total += P3[t, j].astype(F32)
        FIN[t, pl.ds(tile0, T)] = total.astype(BF16)
        start(cp4(t))

    def share5(t):
        arrived(cp4_in(t))
        start(cp5(t))

    def share6(t):
        arrived(cp5_in(t))
        start(cp6(t))

    def finish(t):
        arrived(cp6_in(t))
        return pltpu.make_async_copy(FIN.at[t], fin_hbm.at[t], out_sem.at[t])

    loss1 = [remote(L0, L1, ls.at[0], lr.at[0], (r, partner))]
    loss2 = [remote(L2.at[0], L2.at[j], ls.at[j], lr.at[j], (r, lax.rem(chip + j, C2) * 2 + core))
             for j in range(1, C2)]
    loss3 = [remote(L3.at[0], L3.at[j], ls.at[C2 - 1 + j], lr.at[C2 - 1 + j], (lax.rem(r + j, R), c))
             for j in range(1, R)]

    if square:
        start(loss1)
        user_part(0, put_kept)
        user_home.wait_recv()
        backward_in(
            1, lambda s: (GU[0, s, :] + RL[1, s, :].astype(F32)).astype(BF16).astype(F32)
        )
        backward_out(1)
        start(cp1(1))
        arrived(loss1)
        L2[0] = L0[...] + L1[...]
        start(loss2)
        sum1(1)
        near_home.wait_recv()

        @pl.when(inner)
        def _():
            buddy_home.wait_recv()

        backward_in(
            0,
            lambda s: (RR[0, s, :].astype(F32) + RR[1, s, :].astype(F32)).astype(BF16).astype(F32),
        )
    else:
        start(loss1)
        relay(0)
        lax.fori_loop(0, R, user_grad, 0)
        if R > 2:
            relay(1)
        backward_in(1, lambda s: GU[0, s, :].astype(BF16).astype(F32))
        if R > 3:
            relay(2)
        backward_out(1)
        start(cp1(1))
        for k in range(3, R - 1):
            relay(k)
        arrived(loss1)
        L2[0] = L0[...] + L1[...]
        start(loss2)

        @pl.when(r > 0)
        def _():
            rs(r, True).wait_recv()

        sum1(1)

        @pl.when(r < R - 1)
        def _():
            rs(r, False).wait_recv()

        has_left = jnp.where(r > 0, 1.0, 0.0)
        has_right = jnp.where(r < R - 1, 1.0, 0.0)

        @pl.when(r > 0)
        def _():
            add_rows(GI, r, RR)

        @pl.when(r < R - 1)
        def _():
            add_rows(GI, r, RL)

        backward_in(0, lambda s: GI[r, s, :].astype(F32))
    sum2(1)
    backward_out(0)
    start(cp1(0))
    arrived(loss2)
    L3[0] = functools.reduce(lambda a, b: a + b, [L2[j] for j in range(C2)])
    start(loss3)
    sum3(1)
    sum1(0)
    share5(1)
    sum2(0)
    share6(1)
    sum3(0)
    out1 = finish(1)
    out1.start()
    share5(0)
    arrived(loss3)
    loss_ref[...] = functools.reduce(lambda a, b: a + b, [L3[j] for j in range(R)])
    share6(0)
    out0 = finish(0)
    out0.start()

    if square:

        @pl.when(inner)
        def _():
            for cp in (item_near, item_buddy, far_home, near_home):
                cp.wait_send()

        @pl.when(outer)
        def _():
            item_far.wait_send()
            buddy_home.wait_send()

        for cp in (user_out, scale_out, place_out, swap, user_home):
            cp.wait_send()
    else:

        def sent(b, _):
            @pl.when(jnp.logical_and(r < R - 1, b <= r))
            def _():
                ag(b, True).wait_send()

            @pl.when(jnp.logical_and(r > 0, b >= r))
            def _():
                ag(b, False).wait_send()

            @pl.when(b > r)
            def _():
                rs(b, True).wait_send()

            @pl.when(b < r)
            def _():
                rs(b, False).wait_send()

            return 0

        lax.fori_loop(0, R, sent, 0)
    for t in range(2):
        for cps in (cp1(t), cp2(t), cp3(t), cp4(t), cp5(t), cp6(t)):
            for cp in cps:
                cp.wait_send()
    for cp in loss1 + loss2 + loss3:
        cp.wait_send()
    out1.wait()
    out0.wait()


def block_at(t, start, i):
    return (t, start + i, 0)


def unpack(n, *refs):
    src, dst = list(refs[:n]), refs[n:]
    for out in dst:
        for k in range(out.shape[1] // 128):
            out[:, k * 128 : (k + 1) * 128] = src.pop(0)[0].astype(F32)


def solution(mesh):
    R, C = mesh.shape["row"], mesh.shape["col"]
    C2 = C // 2

    def body(xu, xi, sharp, pos, w1u, w2u, w1i, w2i):
        M, F = xu.shape
        H, E = w2u.shape
        tiles = (F // 16) * (H // 128) + (H // 16) * (E // 128)
        T = -(-tiles // (R * C))
        NT = T * R * C
        RT = R * T
        hold = R * M * M * 4 <= 1 << 24
        V = pltpu.VMEM
        DMA = pltpu.SemaphoreType.DMA
        hbm = pl.BlockSpec(memory_space=pl.ANY)
        vmem = pl.BlockSpec(memory_space=pltpu.VMEM)
        fin, loss = pl.pallas_call(
            functools.partial(kernel, R, C, T, M, F, H, E, hold),
            name="step",
            out_shape=(
                jax.ShapeDtypeStruct((2, NT, 16, 128), BF16),
                jax.ShapeDtypeStruct((8, 128), F32),
            ),
            in_specs=[hbm, hbm, vmem, vmem, hbm, hbm, hbm, hbm],
            out_specs=(hbm, vmem),
            scratch_shapes=[
                V((2, M, F), BF16), V((2, F, H), BF16), V((2, H, E), BF16),
                V((2, M, H), BF16), V((2, M, E), F32), V((2, M, E), BF16),
                V((R, M, E), BF16), V((R, M, M) if hold else (1, 8, 128), F32), V((R, M, M), BF16),
                V((R, M, E), BF16), V((R, M, E), BF16), V((R, M, E), BF16),
                V((2, M, E), F32), V((M, E), BF16), V((M, H), BF16),
                V((1, M), F32), V((1, M), F32),
                V((2, NT, 16, 128), BF16), V((2, NT // 2, 16, 128), BF16),
                V((2, C2 - 1, RT, 16, 128), BF16), V((2, RT, 16, 128), BF16),
                V((2, R - 1, T, 16, 128), BF16), V((2, NT, 16, 128), BF16),
                V((8, 128), F32), V((8, 128), F32), V((C2, 8, 128), F32), V((R, 8, 128), F32),
                V((2, 1, M), F32), V((2, 1, M), jnp.int32), V((4, 1, M), F32), V((4, 1, M), F32),
                DMA((2, 3)), DMA((2,)), DMA((2, R)), DMA((R,)), DMA((R,)), DMA((2, R)),
                DMA((2,)), DMA((2,)), DMA((2, C2 - 1)), DMA((2, C2 - 1)),
                DMA((2, R - 1)), DMA((2, R - 1)), DMA((2, R - 1)), DMA((2, R - 1)),
                DMA((2, C2 - 1)), DMA((2, C2 - 1)), DMA((2,)), DMA((2,)),
                DMA((C2 + R,)), DMA((C2 + R,)), DMA((11,)), DMA((11,)),
            ],
            compiler_params=pltpu.CompilerParams(
                collective_id=0, has_side_effects=True, vmem_limit_bytes=67043328
            ),
        )(xu, xi, sharp[None, :], pos[None, :], w1u, w2u, w1i, w2i)

        flat = fin.reshape(2, NT * 16, 128)
        steps = 4
        specs, outs, shapes = [], [], []
        for t in range(2):
            base = 0
            for height, width in ((F, H), (H, E)):
                tall = height // steps
                for k in range(width // 128):
                    start = (base + k * height) // tall
                    specs.append(
                        pl.BlockSpec((1, tall, 128), functools.partial(block_at, t, start))
                    )
                base += height * (width // 128)
                outs.append(pl.BlockSpec((tall, width), lambda i: (i, 0)))
                shapes.append(jax.ShapeDtypeStruct((height, width), F32))
        i1, i2, u1, u2 = pl.pallas_call(
            functools.partial(unpack, len(specs)),
            name="unpack",
            grid=(steps,),
            in_specs=specs,
            out_specs=outs,
            out_shape=shapes,
        )(*([flat] * len(specs)))
        return (loss[0, 0] / (M * R * C), u1, u2, i1, i2)

    placed = (
        P(("row", "col"), None), P(("row", "col"), None), P(("row", "col")), P(("row", "col")),
        P(), P(), P(), P(),
    )
    return jax.shard_map(
        body, mesh=mesh, in_specs=placed, out_specs=(P(), P(), P(), P(), P()), check_vma=False
    )
```

```python
import functools

import jax
import jax.numpy as jnp
from jax import lax
from jax.experimental import pallas as pl
from jax.experimental.pallas import tpu as pltpu
from jax.sharding import PartitionSpec as P

EPS = 1e-06
MESH = pl.DeviceIdType.MESH
F32 = jnp.float32
BF16 = jnp.bfloat16
TILE = 256


def mm(a, b, ca=1, cb=0):
    return lax.dot_general(a, b, (((ca,), (cb,)), ((), ())), preferred_element_type=F32)


def kernel(
    R, C, T, M, F, H, E, hold,
    xu_hbm, xi_hbm, sharp_ref, pos_ref, w1u_hbm, w2u_hbm, w1i_hbm, w2i_hbm,
    fin_hbm, loss_ref,
    X, W1, W2, HID, OUT, U, IT, EX, D, GI, RR, RL, GU, GV, GP, LS, PK,
    B, P1, P2, S2, P3, FIN, L0, L1, L2, L3, FS, PS, SUMS, OTHER,
    in_sem, out_sem, ag_send, ag_recv, rs_send, rs_recv,
    c1s, c1r, c2s, c2r, c3s, c3r, c4s, c4r, c5s, c5r, c6s, c6r, ls, lr, sq_send, sq_recv,
):
    C2 = C // 2
    square = R == 4 and hold
    r = lax.axis_index("row")
    c = lax.axis_index("col")
    core = lax.rem(c, 2)
    chip = c // 2
    partner = chip * 2 + (1 - core)
    NH = C2 * R * T
    NT = 2 * NH
    RT = R * T
    loads = []
    for t, (xh, w1h, w2h) in enumerate(((xi_hbm, w1i_hbm, w2i_hbm), (xu_hbm, w1u_hbm, w2u_hbm))):
        for k, (src, dst) in enumerate(((w1h, W1.at[t]), (w2h, W2.at[t]), (xh, X.at[t]))):
            loads.append(pltpu.make_async_copy(src, dst, in_sem.at[t, k]))
    for cp in loads:
        cp.start()

    barrier = pltpu.get_barrier_semaphore()
    for j in range(1, R):
        pl.semaphore_signal(barrier, inc=1, device_id=(lax.rem(r + j, R), c), device_id_type=MESH)
    for j in range(1, C2):
        pl.semaphore_signal(
            barrier, inc=1, device_id=(r, lax.rem(chip + j, C2) * 2 + core), device_id_type=MESH
        )
    pl.semaphore_signal(barrier, inc=1, device_id=(r, partner), device_id_type=MESH)

    def rows(i):
        return pl.ds(pl.multiple_of(i * TILE, TILE), TILE)

    def forward(t, put):
        def step(i, _):
            s = rows(i)
            pre = mm(X[t, s, :], W1[t])
            h = jnp.maximum(pre, 0.0).astype(BF16)
            HID[t, s, :] = h
            out = mm(h, W2[t])
            OUT[t, s, :] = out
            inv = lax.rsqrt(jnp.mean(out * out, axis=-1, keepdims=True) + EPS)
            put(s, (out * inv).astype(BF16))
            return 0

        lax.fori_loop(0, M // TILE, step, 0)

    for cp in loads[:3]:
        cp.wait()

    def put_item(s, v):
        IT[0 if square else r, s, :] = v

    forward(0, put_item)
    pl.semaphore_wait(barrier, R + C2 - 1)

    if square:
        inner = jnp.logical_or(r == 1, r == 2)
        outer = jnp.logical_not(inner)
        side = r // 2
        buddy = side * 2 + (1 - lax.rem(r, 2))
        across = 2 - side
        beyond = 3 - 3 * side
        first_slot = jnp.where(inner, 1, 0)

        def block_of(slot):
            near = jnp.where(inner, across, buddy)
            return jnp.where(slot == 0, r, jnp.where(slot == 1, near, beyond))

        def to(src, dst, k, row, ks=None):
            return pltpu.make_async_remote_copy(
                src_ref=src, dst_ref=dst, send_sem=sq_send.at[k if ks is None else ks], recv_sem=sq_recv.at[k],
                device_id=(row, c), device_id_type=MESH,
            )

        item_near = to(IT.at[0], IT.at[1], 0, across)
        item_buddy = to(IT.at[0], IT.at[1], 1, buddy)
        item_far = to(IT.at[0], IT.at[2], 2, across)
        user_out = to(U.at[0], U.at[1], 3, buddy)
        scale_out = to(FS.at[0], FS.at[1], 4, buddy)
        place_out = to(PS.at[0], PS.at[1], 5, buddy)

        @pl.when(inner)
        def _():
            item_near.start()
            item_buddy.start()

        @pl.when(outer)
        def _():
            item_far.start()

        FS[0] = sharp_ref[...].astype(F32) * (1.0 / E)
        PS[0] = pos_ref[...]
        for cp in loads[3:]:
            cp.wait()

        def put_user(s, v):
            U[0, s, :] = v

        forward(1, put_user)
        user_out.start()
        scale_out.start()
        place_out.start()
        SUMS[...] = jnp.zeros_like(SUMS)

        def score(q, slot):
            b = block_of(slot)
            pair = q * 2 + slot - first_slot
            factor = FS[q]
            positive = PS[q]

            def step(i, _):
                s = rows(i)
                logit = mm(IT[slot, s, :], U[q], 1, 1) * factor
                item = lax.broadcasted_iota(jnp.int32, logit.shape, 0) + (b * M + i * TILE)
                e = jnp.exp(logit)
                EX[pair, s, :] = e
                SUMS[q] += jnp.sum(e, axis=0, keepdims=True)
                SUMS[2 + q] += jnp.sum(
                    jnp.where(item == positive, logit, 0.0), axis=0, keepdims=True
                )
                return 0

            lax.fori_loop(0, M // TILE, step, 0)

        @pl.when(outer)
        def _():
            score(0, 0)
            item_buddy.wait_recv()

        @pl.when(inner)
        def _():
            item_near.wait_recv()

        score(0, 1)
        scale_out.wait_recv()
        place_out.wait_recv()
        user_out.wait_recv()
        score(1, 1)

        @pl.when(outer)
        def _():
            score(1, 0)

        @pl.when(inner)
        def _():
            item_far.wait_recv()

            def both(q, _):
                score(q, 2)
                return 0

            lax.fori_loop(0, 2, both, 0)

        swap = to(SUMS, OTHER, 6, buddy)
        swap.start()
        swap.wait_recv()
        total0 = SUMS[0] + OTHER[1]
        total1 = SUMS[1] + OTHER[0]
        L0[...] = jnp.full(L0.shape, jnp.sum(jnp.log(total0) - (SUMS[2] + OTHER[3])), F32)
        NORM = (1.0 / total0, 1.0 / total1)

        def back(q, k):
            b = block_of(first_slot + k)
            rate = FS[q] * (1.0 / M)
            positive = PS[q]

            def step(i, _):
                s = rows(i)
                item = lax.broadcasted_iota(jnp.int32, (TILE, M), 0) + (b * M + i * TILE)
                hit = jnp.where(item == positive, 1.0, 0.0)
                D[2 * q + k, s, :] = ((EX[2 * q + k, s, :] * NORM[q] - hit) * rate).astype(BF16)
                return 0

            lax.fori_loop(0, M // TILE, step, 0)

        def user_part(q, put):
            def step(i, _):
                s = rows(i)
                put(s, mm(D[2 * q, :, s], IT[first_slot], 0, 0)
                    + mm(D[2 * q + 1, :, s], IT[first_slot + 1], 0, 0))
                return 0

            lax.fori_loop(0, M // TILE, step, 0)

        def put_sent(s, v):
            RL[0, s, :] = v.astype(BF16)

        def put_kept(s, v):
            GU[0, s, :] = v

        user_home = to(RL.at[0], RL.at[1], 7, buddy)
        back(1, 0)
        back(1, 1)
        user_part(1, put_sent)
        user_home.start()
        back(0, 0)
        back(0, 1)

        def item_part(k):
            def step(i, _):
                s = rows(i)
                GI[k, s, :] = (mm(D[k, s, :], U[0]) + mm(D[2 + k, s, :], U[1])).astype(BF16)
                return 0

            lax.fori_loop(0, M // TILE, step, 0)

        far_home = to(GI.at[1], RR.at[0], 8, beyond, 10)
        near_home = to(GI.at[0], RR.at[0], 8, across)
        buddy_home = to(GI.at[1], RR.at[1], 9, buddy)
        item_part(1)

        @pl.when(inner)
        def _():
            far_home.start()

        @pl.when(outer)
        def _():
            buddy_home.start()

        item_part(0)

        @pl.when(inner)
        def _():
            near_home.start()

        @pl.when(outer)
        def _():
            RR[1] = GI[0]

    else:

        def ag(b, right):
            d = 1 if right else 0
            return pltpu.make_async_remote_copy(
                src_ref=IT.at[b], dst_ref=IT.at[b], send_sem=ag_send.at[d, b], recv_sem=ag_recv.at[b],
                device_id=(r + 1 if right else r - 1, c), device_id_type=MESH,
            )

        @pl.when(r < R - 1)
        def _():
            ag(r, True).start()

        @pl.when(r > 0)
        def _():
            ag(r, False).start()

        for cp in loads[3:]:
            cp.wait()

        def put_user(s, v):
            U[0, s, :] = v

        forward(1, put_user)
        LS[...] = jnp.zeros_like(LS)
        PK[...] = jnp.zeros_like(PK)
        factor = sharp_ref[...].astype(F32) * (1.0 / E)
        positive = pos_ref[...]

        def score(b):
            def step(i, _):
                s = rows(i)
                logit = mm(IT[b, s, :], U[0], 1, 1) * factor
                item = lax.broadcasted_iota(jnp.int32, logit.shape, 0) + (b * M + i * TILE)
                e = jnp.exp(logit)
                if hold:
                    EX[b, s, :] = e
                LS[...] += jnp.sum(e, axis=0, keepdims=True)
                PK[...] += jnp.sum(jnp.where(item == positive, logit, 0.0), axis=0, keepdims=True)
                return 0

            lax.fori_loop(0, M // TILE, step, 0)

        score(r)

        def arrive(d, _):
            lo = r - d
            hi = r + d

            @pl.when(lo >= 0)
            def _():
                ag(lo, True).wait_recv()

                @pl.when(r < R - 1)
                def _():
                    ag(lo, True).start()

            @pl.when(hi < R)
            def _():
                ag(hi, False).wait_recv()

                @pl.when(r > 0)
                def _():
                    ag(hi, False).start()

            def one(k, _):
                b = lo + k * (hi - lo)

                @pl.when(jnp.logical_and(b >= 0, b < R))
                def _():
                    score(b)

                return 0

            lax.fori_loop(0, 2, one, 0)
            return 0

        lax.fori_loop(1, R, arrive, 0)

        L0[...] = jnp.full(L0.shape, jnp.sum(jnp.log(LS[...]) - PK[...]), F32)
        GU[0] = jnp.zeros((M, E), F32)
        rate = factor * (1.0 / M)
        norm = 1.0 / LS[...]

        def back(b):
            def step(i, _):
                s = rows(i)
                item = lax.broadcasted_iota(jnp.int32, (TILE, M), 0) + (b * M + i * TILE)
                hit = jnp.where(item == positive, 1.0, 0.0)
                e = EX[b, s, :] if hold else jnp.exp(mm(IT[b, s, :], U[0], 1, 1) * factor)
                d = ((e * norm - hit) * rate).astype(BF16)
                D[b, s, :] = d
                GI[b, s, :] = mm(d, U[0]).astype(BF16)
                return 0

            lax.fori_loop(0, M // TILE, step, 0)

        def rs(b, right):
            d = 1 if right else 0
            land = RR if right else RL
            return pltpu.make_async_remote_copy(
                src_ref=GI.at[b], dst_ref=land.at[b], send_sem=rs_send.at[b], recv_sem=rs_recv.at[d, b],
                device_id=(r + 1 if right else r - 1, c), device_id_type=MESH,
            )

        def leave(k, _):
            d = R - 1 - k
            lo = r - d
            hi = r + d

            def one(q, _):
                b = hi + q * (lo - hi)

                @pl.when(jnp.logical_and(b >= 0, b < R))
                def _():
                    back(b)

                return 0

            lax.fori_loop(0, 2, one, 0)

            @pl.when(jnp.logical_and(hi < R, r == 0))
            def _():
                rs(hi, True).start()

            @pl.when(jnp.logical_and(lo >= 0, r == R - 1))
            def _():
                rs(lo, False).start()

            return 0

        lax.fori_loop(0, R - 1, leave, 0)

        def add_rows(dst, b, land):
            def step(i, _):
                s = rows(i)
                dst[b, s, :] = (dst[b, s, :].astype(F32) + land[b, s, :].astype(F32)).astype(BF16)
                return 0

            lax.fori_loop(0, M // TILE, step, 0)

        def relay(k):
            hi = R - 1 - k
            lo = k

            @pl.when(jnp.logical_and(hi > r, r > 0))
            def _():
                rs(hi, True).wait_recv()
                add_rows(GI, hi, RR)
                rs(hi, True).start()

            @pl.when(jnp.logical_and(lo < r, r < R - 1))
            def _():
                rs(lo, False).wait_recv()
                add_rows(GI, lo, RL)
                rs(lo, False).start()

        back(r)

        def user_grad(b, _):
            def step(i, _):
                s = rows(i)
                GU[0, s, :] += mm(D[b, :, s], IT[b], 0, 0)
                return 0

            lax.fori_loop(0, M // TILE, step, 0)
            return 0

    def backward_in(t, grad):
        def step(i, _):
            s = rows(i)
            g = grad(s)
            out = OUT[t, s, :]
            inv = lax.rsqrt(jnp.mean(out * out, axis=-1, keepdims=True) + EPS)
            n = out * inv
            go = (inv * (g - n * jnp.mean(g * n, axis=-1, keepdims=True))).astype(BF16)
            GV[s, :] = go
            gh = mm(go, W2[t], 1, 1)
            GP[s, :] = jnp.where(HID[t, s, :].astype(F32) > 0, gh, 0.0).astype(BF16)
            return 0

        lax.fori_loop(0, M // TILE, step, 0)

    def lay(t, base, height, i, v):
        for k in range(v.shape[1] // 128):
            part = v[:, k * 128 : (k + 1) * 128].astype(BF16).reshape(TILE // 16, 16, 128)
            B[t, pl.ds(base + k * (height // 16) + i * (TILE // 16), TILE // 16)] = part

    def backward_out(t):
        def second(i, _):
            lay(t, (F // 16) * (H // 128), H, i, mm(HID[t, :, rows(i)], GV[...], 0, 0))
            return 0

        lax.fori_loop(0, H // TILE, second, 0)

        def first(i, _):
            lay(t, 0, F, i, mm(X[t, :, rows(i)], GP[...], 0, 0))
            return 0

        lax.fori_loop(0, F // TILE, first, 0)

    def remote(src, dst, ss, rr, dev):
        return pltpu.make_async_remote_copy(
            src_ref=src, dst_ref=dst, send_sem=ss, recv_sem=rr, device_id=dev, device_id_type=MESH
        )

    half = core * NH
    mine = half + chip * RT
    tile0 = mine + r * T

    def cp1(t):
        return [remote(B.at[t, pl.ds((1 - core) * NH, NH)], P1.at[t], c1s.at[t], c1r.at[t], (r, partner))]

    def cp2(t):
        out = []
        for j in range(1, C2):
            to = lax.rem(chip + j, C2)
            out.append(remote(B.at[t, pl.ds(half + to * RT, RT)], P2.at[t, j - 1], c2s.at[t, j - 1],
                              c2r.at[t, j - 1], (r, to * 2 + core)))
        return out

    def cp3(t):
        out = []
        for j in range(1, R):
            to = lax.rem(r + j, R)
            out.append(remote(S2.at[t, pl.ds(to * T, T)], P3.at[t, j - 1], c3s.at[t, j - 1],
                              c3r.at[t, j - 1], (to, c)))
        return out

    def cp4(t):
        ref = FIN.at[t, pl.ds(tile0, T)]
        return [remote(ref, ref, c4s.at[t, j - 1], c4r.at[t, j - 1], (lax.rem(r + j, R), c))
                for j in range(1, R)]

    def cp4_in(t):
        out = []
        for j in range(1, R):
            ref = FIN.at[t, pl.ds(mine + lax.rem(r + R - j, R) * T, T)]
            out.append(remote(ref, ref, c4s.at[t, j - 1], c4r.at[t, j - 1], (lax.rem(r + j, R), c)))
        return out

    def cp5(t):
        ref = FIN.at[t, pl.ds(mine, RT)]
        return [remote(ref, ref, c5s.at[t, j - 1], c5r.at[t, j - 1],
                       (r, lax.rem(chip + j, C2) * 2 + core)) for j in range(1, C2)]

    def cp5_in(t):
        out = []
        for j in range(1, C2):
            ref = FIN.at[t, pl.ds(half + lax.rem(chip + C2 - j, C2) * RT, RT)]
            out.append(remote(ref, ref, c5s.at[t, j - 1], c5r.at[t, j - 1],
                              (r, lax.rem(chip + j, C2) * 2 + core)))
        return out

    def cp6(t):
        ref = FIN.at[t, pl.ds(half, NH)]
        return [remote(ref, ref, c6s.at[t], c6r.at[t], (r, partner))]

    def cp6_in(t):
        ref = FIN.at[t, pl.ds((1 - core) * NH, NH)]
        return [remote(ref, ref, c6s.at[t], c6r.at[t], (r, partner))]

    def start(cps):
        for cp in cps:
            cp.start()

    def arrived(cps):
        for cp in cps:
            cp.wait_recv()

    def sum1(t):
        arrived(cp1(t))

        def step(i, _):
            at = pl.ds(half + i * RT, RT)
            B[t, at] = (B[t, at].astype(F32) + P1[t, pl.ds(i * RT, RT)].astype(F32)).astype(BF16)
            return 0

        lax.fori_loop(0, C2, step, 0)
        start(cp2(t))

    def sum2(t):
        arrived(cp2(t))
        total = B[t, pl.ds(mine, RT)].astype(F32)
        for j in range(C2 - 1):
            total += P2[t, j].astype(F32)
        S2[t] = total.astype(BF16)
        start(cp3(t))

    def sum3(t):
        arrived(cp3(t))
        total = S2[t, pl.ds(r * T, T)].astype(F32)
        for j in range(R - 1):
            total += P3[t, j].astype(F32)
        FIN[t, pl.ds(tile0, T)] = total.astype(BF16)
        start(cp4(t))

    def share5(t):
        arrived(cp4_in(t))
        start(cp5(t))

    def share6(t):
        arrived(cp5_in(t))
        start(cp6(t))

    def finish(t):
        arrived(cp6_in(t))
        return pltpu.make_async_copy(FIN.at[t], fin_hbm.at[t], out_sem.at[t])

    loss1 = [remote(L0, L1, ls.at[0], lr.at[0], (r, partner))]
    loss2 = [remote(L2.at[0], L2.at[j], ls.at[j], lr.at[j], (r, lax.rem(chip + j, C2) * 2 + core))
             for j in range(1, C2)]
    loss3 = [remote(L3.at[0], L3.at[j], ls.at[C2 - 1 + j], lr.at[C2 - 1 + j], (lax.rem(r + j, R), c))
             for j in range(1, R)]

    if square:
        start(loss1)
        user_part(0, put_kept)
        user_home.wait_recv()
        backward_in(
            1, lambda s: (GU[0, s, :] + RL[1, s, :].astype(F32)).astype(BF16).astype(F32)
        )
        backward_out(1)
        start(cp1(1))
        arrived(loss1)
        L2[0] = L0[...] + L1[...]
        start(loss2)
        sum1(1)
        sum2(1)
        near_home.wait_recv()

        @pl.when(inner)
        def _():
            buddy_home.wait_recv()

        backward_in(
            0,
            lambda s: (RR[0, s, :].astype(F32) + RR[1, s, :].astype(F32)).astype(BF16).astype(F32),
        )
    else:
        start(loss1)
        relay(0)
        lax.fori_loop(0, R, user_grad, 0)
        if R > 2:
            relay(1)
        backward_in(1, lambda s: GU[0, s, :].astype(BF16).astype(F32))
        if R > 3:
            relay(2)
        backward_out(1)
        start(cp1(1))
        for k in range(3, R - 1):
            relay(k)
        arrived(loss1)
        L2[0] = L0[...] + L1[...]
        start(loss2)

        @pl.when(r > 0)
        def _():
            rs(r, True).wait_recv()

        sum1(1)

        @pl.when(r < R - 1)
        def _():
            rs(r, False).wait_recv()

        has_left = jnp.where(r > 0, 1.0, 0.0)
        has_right = jnp.where(r < R - 1, 1.0, 0.0)

        @pl.when(r > 0)
        def _():
            add_rows(GI, r, RR)

        @pl.when(r < R - 1)
        def _():
            add_rows(GI, r, RL)

        sum2(1)
        backward_in(0, lambda s: GI[r, s, :].astype(F32))
    sum3(1)
    backward_out(0)
    start(cp1(0))
    arrived(loss2)
    L3[0] = functools.reduce(lambda a, b: a + b, [L2[j] for j in range(C2)])
    start(loss3)
    share5(1)
    sum1(0)
    share6(1)
    sum2(0)
    sum3(0)
    out1 = finish(1)
    out1.start()
    share5(0)
    arrived(loss3)
    loss_ref[...] = functools.reduce(lambda a, b: a + b, [L3[j] for j in range(R)])
    share6(0)
    out0 = finish(0)
    out0.start()

    if square:

        @pl.when(inner)
        def _():
            for cp in (item_near, item_buddy, far_home, near_home):
                cp.wait_send()

        @pl.when(outer)
        def _():
            item_far.wait_send()
            buddy_home.wait_send()

        for cp in (user_out, scale_out, place_out, swap, user_home):
            cp.wait_send()
    else:

        def sent(b, _):
            @pl.when(jnp.logical_and(r < R - 1, b <= r))
            def _():
                ag(b, True).wait_send()

            @pl.when(jnp.logical_and(r > 0, b >= r))
            def _():
                ag(b, False).wait_send()

            @pl.when(b > r)
            def _():
                rs(b, True).wait_send()

            @pl.when(b < r)
            def _():
                rs(b, False).wait_send()

            return 0

        lax.fori_loop(0, R, sent, 0)
    for t in range(2):
        for cps in (cp1(t), cp2(t), cp3(t), cp4(t), cp5(t), cp6(t)):
            for cp in cps:
                cp.wait_send()
    for cp in loss1 + loss2 + loss3:
        cp.wait_send()
    out1.wait()
    out0.wait()


def block_at(t, start, i):
    return (t, start + i, 0)


def unpack(n, *refs):
    src, dst = list(refs[:n]), refs[n:]
    for out in dst:
        for k in range(out.shape[1] // 128):
            out[:, k * 128 : (k + 1) * 128] = src.pop(0)[0].astype(F32)


def solution(mesh):
    R, C = mesh.shape["row"], mesh.shape["col"]
    C2 = C // 2

    def body(xu, xi, sharp, pos, w1u, w2u, w1i, w2i):
        M, F = xu.shape
        H, E = w2u.shape
        tiles = (F // 16) * (H // 128) + (H // 16) * (E // 128)
        T = -(-tiles // (R * C))
        NT = T * R * C
        RT = R * T
        hold = R * M * M * 4 <= 1 << 24
        V = pltpu.VMEM
        DMA = pltpu.SemaphoreType.DMA
        hbm = pl.BlockSpec(memory_space=pl.ANY)
        vmem = pl.BlockSpec(memory_space=pltpu.VMEM)
        fin, loss = pl.pallas_call(
            functools.partial(kernel, R, C, T, M, F, H, E, hold),
            name="step",
            out_shape=(
                jax.ShapeDtypeStruct((2, NT, 16, 128), BF16),
                jax.ShapeDtypeStruct((8, 128), F32),
            ),
            in_specs=[hbm, hbm, vmem, vmem, hbm, hbm, hbm, hbm],
            out_specs=(hbm, vmem),
            scratch_shapes=[
                V((2, M, F), BF16), V((2, F, H), BF16), V((2, H, E), BF16),
                V((2, M, H), BF16), V((2, M, E), F32), V((2, M, E), BF16),
                V((R, M, E), BF16), V((R, M, M) if hold else (1, 8, 128), F32), V((R, M, M), BF16),
                V((R, M, E), BF16), V((R, M, E), BF16), V((R, M, E), BF16),
                V((2, M, E), F32), V((M, E), BF16), V((M, H), BF16),
                V((1, M), F32), V((1, M), F32),
                V((2, NT, 16, 128), BF16), V((2, NT // 2, 16, 128), BF16),
                V((2, C2 - 1, RT, 16, 128), BF16), V((2, RT, 16, 128), BF16),
                V((2, R - 1, T, 16, 128), BF16), V((2, NT, 16, 128), BF16),
                V((8, 128), F32), V((8, 128), F32), V((C2, 8, 128), F32), V((R, 8, 128), F32),
                V((2, 1, M), F32), V((2, 1, M), jnp.int32), V((4, 1, M), F32), V((4, 1, M), F32),
                DMA((2, 3)), DMA((2,)), DMA((2, R)), DMA((R,)), DMA((R,)), DMA((2, R)),
                DMA((2,)), DMA((2,)), DMA((2, C2 - 1)), DMA((2, C2 - 1)),
                DMA((2, R - 1)), DMA((2, R - 1)), DMA((2, R - 1)), DMA((2, R - 1)),
                DMA((2, C2 - 1)), DMA((2, C2 - 1)), DMA((2,)), DMA((2,)),
                DMA((C2 + R,)), DMA((C2 + R,)), DMA((11,)), DMA((11,)),
            ],
            compiler_params=pltpu.CompilerParams(
                collective_id=0, has_side_effects=True, vmem_limit_bytes=67043328
            ),
        )(xu, xi, sharp[None, :], pos[None, :], w1u, w2u, w1i, w2i)

        flat = fin.reshape(2, NT * 16, 128)
        steps = 4
        specs, outs, shapes = [], [], []
        for t in range(2):
            base = 0
            for height, width in ((F, H), (H, E)):
                tall = height // steps
                for k in range(width // 128):
                    start = (base + k * height) // tall
                    specs.append(
                        pl.BlockSpec((1, tall, 128), functools.partial(block_at, t, start))
                    )
                base += height * (width // 128)
                outs.append(pl.BlockSpec((tall, width), lambda i: (i, 0)))
                shapes.append(jax.ShapeDtypeStruct((height, width), F32))
        i1, i2, u1, u2 = pl.pallas_call(
            functools.partial(unpack, len(specs)),
            name="unpack",
            grid=(steps,),
            in_specs=specs,
            out_specs=outs,
            out_shape=shapes,
        )(*([flat] * len(specs)))
        return (loss[0, 0] / (M * R * C), u1, u2, i1, i2)

    placed = (
        P(("row", "col"), None), P(("row", "col"), None), P(("row", "col")), P(("row", "col")),
        P(), P(), P(), P(),
    )
    return jax.shard_map(
        body, mesh=mesh, in_specs=placed, out_specs=(P(), P(), P(), P(), P()), check_vma=False
    )
```
